32 devices in a mesh: groups: 1, seq: 32 (over z, y, x, core).
Axes of the slice: x: 2, y: 2, z: 4, core: 2. Of those that a mesh axis runs over, the one named last changes fastest.
Arguments:
- tokens: bfloat16 [4096, 1536], P(('groups', 'seq')), may hold values from -6 to 6
- state_rates: float32 [2, 64], replicated, may hold values from -40 to 40, as said below
- coupling: float32 [2, 64], replicated, may hold values from -6 to 6
- in_proj: float32 [2, 64, 1536], replicated, may hold values from -120 to 120
- out_proj: float32 [2, 64, 1536], replicated, may hold values from -0.01171875 to 0.01171875
- skip_gain: float32 [1536], replicated, may hold values from -4 to 4
- mix_weight: bfloat16 [1536, 3072], P('seq'), may hold values from -0.15625 to 0.15625
Outputs:
- glu_output: bfloat16 [4096, 1536], P(('groups', 'seq'))
The draws below stay inside these ranges and needn't reach their ends.
Inputs may be any that keep to these rules, and one draw needn't show every extreme that they name: state_rates[0] is negative, between -12 and -1 / 4096; state_rates[1] lies within -40 to 40.
All inputs are finite; a program needn't handle non-finite values.
Results may differ from the reference program's by a relative error of at most 0.0051.
Values may be sent and summed in bfloat16 or wider, within the bound.
No kernel may reach another device: no remote copies, remote signals or barrier semaphores. Data moves between devices by JAX's collectives and lax.ppermute only.
A program may use at most 64 MiB of HBM per device.

```python
import math
import jax
import jax.numpy as jnp
from jax import lax

H = 1536
N = 64
SEQ_LEN = 4096


def state_law(key):
    base_key = jax.random.fold_in(key, 41)
    key_list = jax.random.split(base_key, 7)
    lowest = 1.0 / SEQ_LEN
    highest = 0.03
    span_log = math.log(highest / lowest)
    offset_log = jax.random.uniform(key_list[1], (N,), jnp.float32) * span_log
    step_decay = lowest * jnp.exp(offset_log)
    turn_angle = jax.random.uniform(key_list[3], (N,), jnp.float32, 0.05, 3.04)
    turn_sign = jnp.where(jax.random.bernoulli(key_list[6], 0.5, (N,)), 1.0, -1.0)
    spin_rate = 2.0 * jnp.tan(0.5 * turn_angle) * turn_sign
    stretch = 1.0 + 0.25 * spin_rate * spin_rate
    decay_rate = step_decay * stretch
    magnitude = jnp.sqrt(decay_rate) * jax.random.uniform(key_list[4], (N,), jnp.float32, 0.5, 1.5)
    phases = jax.random.uniform(key_list[5], (N,), jnp.float32, -math.pi, math.pi)
    return (decay_rate, spin_rate, magnitude * jnp.cos(phases), magnitude * jnp.sin(phases), stretch)


def draw_state_rates(key, part):
    decay_rate, spin_rate, low_real, low_imag, stretch = state_law(key)
    return jnp.stack([-decay_rate, spin_rate]).astype(jnp.float32)


def draw_coupling(key, part):
    decay_rate, spin_rate, low_real, low_imag, stretch = state_law(key)
    return jnp.stack([low_real, low_imag]).astype(jnp.float32)


def draw_in_proj(key, part):
    decay_rate, spin_rate, low_real, low_imag, stretch = state_law(key)
    own_key = jax.random.fold_in(key, 59)
    base = jnp.clip(jax.random.normal(own_key, (2, N, H), jnp.float32), -6.0, 6.0)
    return (base * jnp.sqrt(stretch)[None, :, None]).astype(jnp.float32)


def block_scale(rng, shape, cuts, least, high):
    factor_of, own = 1.0, jax.random.fold_in(rng, 6)
    for dim, blocks in cuts:
        heights = jnp.exp(jax.random.uniform(jax.random.fold_in(own, dim), (blocks,), jnp.float32, least / len(cuts), high / len(cuts)))
        factor_of = factor_of * jnp.repeat(heights, shape[dim] // blocks).reshape([-1 if axis == dim else 1 for axis in range(len(shape))])
    return factor_of


def noise(stream_key, extent, deviation, bound, cuts=(), kind=jnp.bfloat16):
    array = jax.random.normal(stream_key, extent, jnp.float32) * deviation
    if len(cuts) > 0:
        array = block_scale(stream_key, extent, cuts, -0.22, 0.18) * array
    return jnp.clip(array, min=-bound, max=bound).astype(kind)


def setup_inputs(seed: int = 0, part: int = 0) -> dict:
    seeds = jax.random.split(jax.random.key(seed), 8)
    own_keys = jax.random.split(jax.random.fold_in(seeds[7], part), 8)
    return {
        "tokens": noise(own_keys[0], (SEQ_LEN, H), 1.0, 6.0, ((0, 32),)),
        "state_rates": draw_state_rates(jax.random.fold_in(seeds[7], 71), part),
        "coupling": draw_coupling(jax.random.fold_in(seeds[7], 71), part),
        "in_proj": draw_in_proj(jax.random.fold_in(seeds[7], 71), part),
        "out_proj": noise(seeds[4], (2, N, H), (N * SEQ_LEN) ** -0.5, 0.01171875, (), jnp.float32),
        "skip_gain": noise(seeds[5], (H,), 1.0, 4.0, (), jnp.float32),
        "mix_weight": noise(seeds[6], (H, 2 * H), H ** -0.5, 0.15625, ((0, 32),)),
    }


def phase_of(numerator, period):
    wrapped = numerator % period
    wrapped = jnp.where(wrapped > period // 2, wrapped - period, wrapped)
    return wrapped.astype(jnp.float32) * (-2.0 * math.pi / period)


def complex_mul(first, second):
    return (first[0] * second[0] - first[1] * second[1], first[0] * second[1] + first[1] * second[0])


def complex_div(first, second):
    norm_sq = second[0] * second[0] + second[1] * second[1]
    return ((first[0] * second[0] + first[1] * second[1]) / norm_sq, (first[1] * second[0] - first[0] * second[1]) / norm_sq)


def real_form(pair_real, pair_imag):
    upper = jnp.concatenate([pair_real, pair_imag], axis=1)
    lower = jnp.concatenate([-pair_imag, pair_real], axis=1)
    return jnp.concatenate([upper, lower], axis=0)


def cauchy_right(coupling, in_proj, out_proj):
    in_pair = (in_proj[0], in_proj[1])
    out_pair = (out_proj[0], out_proj[1])
    low_pair = (coupling[0][:, None], coupling[1][:, None])
    low_conj = (low_pair[0], -low_pair[1])
    pair_cb = complex_mul(out_pair, in_pair)
    pair_cp = complex_mul(out_pair, low_pair)
    pair_pb = complex_mul(low_conj, in_pair)
    pair_pp = low_pair[0] * low_pair[0] + low_pair[1] * low_pair[1]
    return [real_form(pair_cb[0], pair_cb[1]), real_form(pair_cp[0], pair_cp[1]),
            real_form(pair_pb[0], pair_pb[1]), real_form(pair_pp, jnp.zeros_like(pair_pp))]


def response(frequency, full_len, state_rates, right_list):
    half_turn = 0.5 * phase_of(frequency, full_len)
    cos_half = jnp.cos(half_turn)[:, None]
    sin_half = jnp.sin(half_turn)[:, None]
    decay_rate = -state_rates[0][None, :]
    spin_rate = state_rates[1][None, :]
    real_part = cos_half * decay_rate
    imag_part = -(2.0 * sin_half + cos_half * spin_rate)
    inv_norm = 1.0 / (real_part * real_part + imag_part * imag_part)
    cauchy_left = jnp.concatenate([real_part * inv_norm, -imag_part * inv_norm], axis=1)
    term_list = []
    for matrix in right_list:
        summed = jnp.dot(cauchy_left, matrix, precision=lax.Precision.HIGHEST)
        half_cols = matrix.shape[1] // 2
        term_list.append((summed[:, :half_cols], summed[:, half_cols:]))
    term_cb, term_cp, term_pb, term_pp = term_list
    numerator = complex_mul(term_cp, term_pb)
    denominator = (1.0 + cos_half * term_pp[0], cos_half * term_pp[1])
    fraction = complex_div(numerator, denominator)
    bracket = (term_cb[0] - cos_half * fraction[0], term_cb[1] - cos_half * fraction[1])
    return complex_mul((cos_half, -sin_half), bracket)


def reference(tokens, state_rates, coupling, in_proj, out_proj, skip_gain, mix_weight):
    full_len = 2 * SEQ_LEN
    right_list = cauchy_right(coupling, in_proj, out_proj)
    block_rows = math.gcd(full_len, 4096)
    frequency = jnp.arange(full_len, dtype=jnp.int32).reshape(full_len // block_rows, block_rows)

    def one_block(freq_block):
        kernel_real, kernel_imag = response(freq_block, full_len, state_rates, right_list)
        return jnp.stack([kernel_real, kernel_imag])

    kernels = lax.map(one_block, frequency)
    kernel_real = kernels[:, 0].reshape(full_len, H)
    kernel_imag = kernels[:, 1].reshape(full_len, H)
    signal = tokens.astype(jnp.float32)
    spectrum = jnp.fft.fft(signal, n=full_len, axis=0)
    product = spectrum * lax.complex(kernel_real, kernel_imag)
    conv_out = jnp.real(jnp.fft.ifft(product, axis=0))[:SEQ_LEN]
    pre_act = conv_out + skip_gain[None, :] * signal
    activation = jax.nn.gelu(pre_act, approximate=False).astype(jnp.bfloat16)
    projected = jnp.dot(activation.astype(jnp.float32), mix_weight.astype(jnp.float32), precision=lax.Precision.HIGHEST)
    return (projected[:, :H] * jax.nn.sigmoid(projected[:, H:])).astype(jnp.bfloat16)
```

```python
import functools
import math

import jax
import jax.numpy as jnp
import numpy as np
from jax import lax
from jax.experimental import pallas as pl
from jax.experimental.pallas import tpu as pltpu
from jax.sharding import PartitionSpec as P

F32 = jnp.float32
BF16 = jnp.bfloat16


def padded(count):
    return -(-count // 8) * 8


def group_of(count, most):
    return max(g for g in range(1, most + 1) if count % g == 0)


def half_angles(seq_count, tok_rows):
    full_len = 2 * seq_count * tok_rows
    freq = np.arange(seq_count + 1)[:, None] + 2 * seq_count * np.arange(tok_rows)[None, :]
    wrapped = np.where(freq > full_len // 2, freq - full_len, freq).astype(np.float32)
    half = wrapped * np.float32(-2.0 * math.pi / full_len) * np.float32(0.5)
    half = half.astype(np.float64)
    weight = np.full((seq_count + 1, 1), 2.0)
    weight[0] = weight[-1] = 1.0
    weight = np.broadcast_to(weight / (2.0 * full_len), half.shape)
    return np.stack([np.cos(half), np.sin(half), weight]).astype(np.float32)


def split_table(table):
    high = table.astype(jnp.bfloat16).astype(np.float64)
    return high.astype(np.float32), (table - high).astype(np.float32)


def conv_tables(seq_count, tok_rows):
    pairs = seq_count + 1
    rows = padded(pairs)
    full_len = 2 * seq_count * tok_rows
    outer = 2.0 * np.pi * np.outer(np.arange(pairs), np.arange(seq_count)) / (2 * seq_count)
    first = np.zeros((2 * rows, seq_count))
    first[:pairs] = np.cos(outer)
    first[rows : rows + pairs] = -np.sin(outer)
    first = np.concatenate(split_table(first), 1)
    last = np.zeros((seq_count, 2 * rows))
    last[:, :pairs] = np.cos(outer).T
    last[:, rows : rows + pairs] = -np.sin(outer).T
    turn = 2.0 * np.pi * np.outer(np.arange(pairs), np.arange(tok_rows)) / full_len
    twiddle = np.zeros((2, rows, tok_rows))
    twiddle[0, :pairs] = np.cos(turn)
    twiddle[1, :pairs] = np.sin(turn)
    inner = 2.0 * np.pi * np.outer(np.arange(tok_rows), np.arange(tok_rows)) / tok_rows
    cosine, sine = np.cos(inner), np.sin(inner)
    forward = np.block([[cosine, -sine], [sine, cosine]])
    inverse = np.block([[cosine, sine], [-sine, cosine]])
    return (
        jnp.asarray(first, BF16),
        jnp.asarray(twiddle, F32),
        jnp.asarray(forward, BF16),
        jnp.asarray(inverse, BF16),
        jnp.asarray(last, BF16),
    )


def thirds(value):
    high = value.astype(BF16)
    rest = value - high.astype(F32)
    middle = rest.astype(BF16)
    low = (rest - middle.astype(F32)).astype(BF16)
    return high, middle, low


def response_kernel(chans, group, width, tab_ref, rates_ref, left_ref, out_ref):
    cos_half = tab_ref[0, 0:1, :]
    sin_half = tab_ref[0, 1:2, :]
    weight = tab_ref[0, 2:3, :]
    cos_two = jnp.concatenate([cos_half, cos_half], 1)
    sin_two = jnp.concatenate([sin_half, -sin_half], 1)
    decay = -rates_ref[:, 0:1]
    spin = rates_ref[:, 1:2]
    power = rates_ref[:, 2:3]
    real_part = cos_two * decay
    imag_part = -(2.0 * sin_two + cos_two * spin)
    inv_norm = 1.0 / (real_part * real_part + imag_part * imag_part)
    v_real = real_part * inv_norm
    v_imag = -imag_part * inv_norm
    pp_real = jnp.sum(v_real * power, axis=0, keepdims=True)
    pp_imag = jnp.sum(v_imag * power, axis=0, keepdims=True)
    den_real = 1.0 + cos_two * pp_real
    den_imag = cos_two * pp_imag
    den_inv = cos_two / (den_real * den_real + den_imag * den_imag)
    d_real = den_real * den_inv
    d_imag = -den_imag * den_inv
    v_high, v_mid, v_low = thirds(jnp.concatenate([v_real, v_imag], 0))
    l_high, l_mid, l_low = thirds(left_ref[...])
    right_a = jnp.concatenate([v_high, v_mid], 0)
    right_b = jnp.concatenate([v_low, v_high], 0)

    def sums(index):
        rows = slice(index * chans, (index + 1) * chans)
        high, mid, low = l_high[rows], l_mid[rows], l_low[rows]
        return (
            jnp.dot(jnp.concatenate([high, low], 1), right_b, preferred_element_type=F32)
            + jnp.dot(jnp.concatenate([mid, mid], 1), right_a, preferred_element_type=F32)
            + jnp.dot(jnp.concatenate([high, high], 1), right_a, preferred_element_type=F32)
        )

    cb_real, cb_imag, cp_real, cp_imag, pb_real, pb_imag = [sums(i) for i in range(6)]
    num_real = cp_real * pb_real - cp_imag * pb_imag
    num_imag = cp_real * pb_imag + cp_imag * pb_real
    q_real = cb_real - (num_real * d_real - num_imag * d_imag)
    q_imag = cb_imag - (num_real * d_imag + num_imag * d_real)
    half = group * width
    b_real = (q_real[:, :half] + q_real[:, half:]) * weight
    b_imag = (q_imag[:, :half] - q_imag[:, half:]) * weight
    s_real = b_real * cos_half + b_imag * sin_half
    s_imag = b_imag * cos_half - b_real * sin_half
    for g in range(group):
        cols = slice(g * width, (g + 1) * width)
        out_ref[g, :, :width] = s_real[:, cols]
        out_ref[g, :, width:] = s_imag[:, cols]


def half_spectrum(tables, rates, left, chans, width):
    pairs = tables.shape[1]
    group = group_of(pairs, 6)
    steps = pairs // group
    states = rates.shape[0]
    tables = tables.reshape(3, steps, group * width).transpose(1, 0, 2)
    return pl.pallas_call(
        functools.partial(response_kernel, chans, group, width),
        grid=(steps,),
        in_specs=[
            pl.BlockSpec((1, 3, group * width), lambda i: (i, 0, 0)),
            pl.BlockSpec((states, 3), lambda i: (0, 0)),
            pl.BlockSpec((6 * chans, 2 * states), lambda i: (0, 0)),
        ],
        out_specs=pl.BlockSpec((group, chans, 2 * width), lambda i: (i, 0, 0)),
        out_shape=jax.ShapeDtypeStruct((pairs, chans, 2 * width), F32),
        cost_estimate=pl.CostEstimate(
            flops=pairs * width * chans * states * 48, bytes_accessed=1 << 21, transcendentals=0
        ),
        name="response",
    )(tables, rates, left)


def conv_kernel(
    seq_count, chans, width, per_loop,
    x_ref, s_ref, skip_ref, first_ref, tw_ref, forward_ref, inverse_ref, last_ref,
    out_ref, xf, ar, ai,
):
    pairs = seq_count + 1
    rows = padded(pairs)
    bundle = 4
    for s in range(seq_count):
        xf[s * chans : (s + 1) * chans, :] = x_ref[s].astype(F32)
    tw_cos, tw_sin = tw_ref[0], tw_ref[1]
    for base in range(0, chans, bundle):
        parts = [xf[pl.ds(base + j, seq_count, stride=chans), :] for j in range(bundle)]
        right = jnp.concatenate(parts, 1).astype(BF16)
        right = jnp.concatenate([right, right], 0)
        got = jnp.dot(first_ref[...], right, preferred_element_type=F32)
        for j in range(bundle):
            cols = slice(j * width, (j + 1) * width)
            real, imag = got[:rows, cols], got[rows:, cols]
            ar[pl.ds(base + j, rows, stride=chans), :] = real * tw_cos + imag * tw_sin
            ai[pl.ds(base + j, rows, stride=chans), :] = imag * tw_cos - real * tw_sin

    span = per_loop * chans

    def step(index, carry):
        at = pl.ds(pl.multiple_of(index * span, 8), span)
        left = jnp.concatenate([ar[at, :], ai[at, :]], 1).astype(BF16)
        spec = jnp.dot(left, forward_ref[...], preferred_element_type=F32)
        filt = s_ref[pl.ds(index * per_loop, per_loop)].reshape(span, 2 * width)
        x_r, x_i = spec[:, :width], spec[:, width:]
        f_r, f_i = filt[:, :width], filt[:, width:]
        prod = jnp.concatenate([x_r * f_r - x_i * f_i, x_r * f_i + x_i * f_r], 1)
        back = jnp.dot(prod.astype(BF16), inverse_ref[...], preferred_element_type=F32)
        ar[at, :] = back[:, :width]
        ai[at, :] = back[:, width:]
        return carry

    lax.fori_loop(0, pairs // per_loop, step, 0)

    for base in range(0, chans, bundle):
        parts = []
        for j in range(bundle):
            real = ar[pl.ds(base + j, rows, stride=chans), :]
            imag = ai[pl.ds(base + j, rows, stride=chans), :]
            parts.append(
                jnp.concatenate(
                    [real * tw_cos - imag * tw_sin, imag * tw_cos + real * tw_sin], 0
                )
            )
        right = jnp.concatenate(parts, 1).astype(BF16)
        got = jnp.dot(last_ref[...], right, preferred_element_type=F32)
        for j in range(bundle):
            at = pl.ds(base + j, seq_count, stride=chans)
            skip = skip_ref[base + j : base + j + 1, :]
            xf[at, :] = got[:, j * width : (j + 1) * width] + skip * xf[at, :]
    for s in range(seq_count):
        pre = xf[s * chans : (s + 1) * chans, :]
        act = 0.5 * pre * (1.0 + lax.erf(pre * math.sqrt(0.5)))
        out_ref[s] = act.astype(BF16)


def filtered(columns, spectrum, skip, seq_count, chans, width):
    pairs = seq_count + 1
    tables = conv_tables(seq_count, width)
    per_loop = group_of(pairs, 13)
    return pl.pallas_call(
        functools.partial(conv_kernel, seq_count, chans, width, per_loop),
        out_shape=jax.ShapeDtypeStruct((seq_count, chans, width), BF16),
        scratch_shapes=[
            pltpu.VMEM((seq_count * chans, width), F32),
            pltpu.VMEM((padded(pairs) * chans, width), F32),
            pltpu.VMEM((padded(pairs) * chans, width), F32),
        ],
        cost_estimate=pl.CostEstimate(
            flops=1 << 29, bytes_accessed=1 << 21, transcendentals=1 << 18
        ),
        name="conv",
    )(columns, spectrum, skip, *tables)


def complex_mul(first, second):
    return (
        first[0] * second[0] - first[1] * second[1],
        first[0] * second[1] + first[1] * second[0],
    )


def left_matrix(coupling, in_own, out_own):
    low = (coupling[0][:, None], coupling[1][:, None])
    low_conj = (low[0], -low[1])
    blocks = []
    for first, second in ((out_own, in_own), (out_own, low), (low_conj, in_own)):
        real, imag = complex_mul(first, second)
        blocks.append(jnp.concatenate([real, -imag], 0).T)
        blocks.append(jnp.concatenate([imag, real], 0).T)
    return jnp.concatenate(blocks, 0)


def shards(tokens, state_rates, coupling, in_proj, out_proj, skip_gain, mix_weight):
    seq_count = lax.axis_size("seq")
    place = lax.axis_index("seq")
    width, channels = tokens.shape
    chans = channels // seq_count
    columns = tokens.T.reshape(seq_count, chans, width)
    columns = lax.all_to_all(columns, "seq", 0, 0)
    in_own = lax.dynamic_slice_in_dim(in_proj, place * chans, chans, 2)
    out_own = lax.dynamic_slice_in_dim(out_proj, place * chans, chans, 2)
    skip = lax.dynamic_slice_in_dim(skip_gain, place * chans, chans, 0)[:, None]
    left = left_matrix(coupling, in_own, out_own)
    power = coupling[0] * coupling[0] + coupling[1] * coupling[1]
    rates = jnp.stack([state_rates[0], state_rates[1], power], 1)
    tables = jnp.asarray(half_angles(seq_count, width))
    spectrum = half_spectrum(tables, rates, left, chans, width)
    activation = filtered(columns, spectrum, skip, seq_count, chans, width)
    act = lax.all_to_all(activation, "seq", 0, 0).reshape(channels, width)
    weight = lax.all_gather(mix_weight, "seq", axis=0, tiled=True)
    projected = lax.dot_general(act, weight, (((0,), (0,)), ((), ())), preferred_element_type=F32)
    return (projected[:, :channels] * jax.nn.sigmoid(projected[:, channels:])).astype(BF16)


def solution(mesh):
    placed = (P(("groups", "seq"), None), P(), P(), P(), P(), P(), P("seq", None))
    return jax.shard_map(
        shards, mesh=mesh, in_specs=placed, out_specs=P(("groups", "seq"), None), check_vma=False
    )
```

```python
import functools
import math

import jax
import jax.numpy as jnp
import numpy as np
from jax import lax
from jax.experimental import pallas as pl
from jax.experimental.pallas import tpu as pltpu
from jax.sharding import Mesh, PartitionSpec as P


F32 = jnp.float32
BF16 = jnp.bfloat16


def padded(count):
    return -(-count // 8) * 8


def group_of(count, most):
    return max(g for g in range(1, most + 1) if count % g == 0)


def half_angles(seq_count, tok_rows):
    full_len = 2 * seq_count * tok_rows
    freq = np.arange(seq_count + 1)[:, None] + 2 * seq_count * np.arange(tok_rows)[None, :]
    wrapped = np.where(freq > full_len // 2, freq - full_len, freq).astype(np.float32)
    half = wrapped * np.float32(-2.0 * math.pi / full_len) * np.float32(0.5)
    half = half.astype(np.float64)
    weight = np.full((seq_count + 1, 1), 2.0)
    weight[0] = weight[-1] = 1.0
    weight = np.broadcast_to(weight / (2.0 * full_len), half.shape)
    return np.stack([np.cos(half), np.sin(half), weight]).astype(np.float32)


def split_table(table):
    high = table.astype(jnp.bfloat16).astype(np.float64)
    return high.astype(np.float32), (table - high).astype(np.float32)


def conv_tables(seq_count, tok_rows):
    pairs = seq_count + 1
    rows = padded(pairs)
    full_len = 2 * seq_count * tok_rows
    outer = 2.0 * np.pi * np.outer(np.arange(pairs), np.arange(seq_count)) / (2 * seq_count)
    first = np.zeros((2 * rows, seq_count))
    first[:pairs] = np.cos(outer)
    first[rows : rows + pairs] = -np.sin(outer)
    first = np.concatenate(split_table(first), 1)
    last = np.zeros((seq_count, 2 * rows))
    last[:, :pairs] = np.cos(outer).T
    last[:, rows : rows + pairs] = -np.sin(outer).T
    turn = 2.0 * np.pi * np.outer(np.arange(pairs), np.arange(tok_rows)) / full_len
    twiddle = np.zeros((2, rows, tok_rows))
    twiddle[0, :pairs] = np.cos(turn)
    twiddle[1, :pairs] = np.sin(turn)
    inner = 2.0 * np.pi * np.outer(np.arange(tok_rows), np.arange(tok_rows)) / tok_rows
    cosine, sine = np.cos(inner), np.sin(inner)
    forward = np.block([[cosine, -sine], [sine, cosine]])
    inverse = np.block([[cosine, sine], [-sine, cosine]])
    return (
        jnp.asarray(first, BF16),
        jnp.asarray(twiddle, F32),
        jnp.asarray(forward, BF16),
        jnp.asarray(inverse, BF16),
        jnp.asarray(last, BF16),
    )


def thirds(value):
    high = value.astype(BF16)
    rest = value - high.astype(F32)
    middle = rest.astype(BF16)
    low = (rest - middle.astype(F32)).astype(BF16)
    return high, middle, low


def response_kernel(chans, group, width, tab_ref, rates_ref, left_ref, out_ref):
    cos_half = tab_ref[0, 0:1, :]
    sin_half = tab_ref[0, 1:2, :]
    weight = tab_ref[0, 2:3, :]
    cos_two = jnp.concatenate([cos_half, cos_half], 1)
    sin_two = jnp.concatenate([sin_half, -sin_half], 1)
    decay = -rates_ref[:, 0:1]
    spin = rates_ref[:, 1:2]
    power = rates_ref[:, 2:3]
    real_part = cos_two * decay
    imag_part = -(2.0 * sin_two + cos_two * spin)
    inv_norm = 1.0 / (real_part * real_part + imag_part * imag_part)
    v_real = real_part * inv_norm
    v_imag = -imag_part * inv_norm
    pp_real = jnp.sum(v_real * power, axis=0, keepdims=True)
    pp_imag = jnp.sum(v_imag * power, axis=0, keepdims=True)
    den_real = 1.0 + cos_two * pp_real
    den_imag = cos_two * pp_imag
    den_inv = cos_two / (den_real * den_real + den_imag * den_imag)
    d_real = den_real * den_inv
    d_imag = -den_imag * den_inv
    v_high, v_mid, v_low = thirds(jnp.concatenate([v_real, v_imag], 0))
    l_high, l_mid, l_low = thirds(left_ref[...])
    right_a = jnp.concatenate([v_high, v_mid], 0)
    right_b = jnp.concatenate([v_low, v_high], 0)

    left_b = jnp.concatenate([l_high, l_low], 1)
    left_a = jnp.concatenate(
        [jnp.concatenate([l_mid, l_mid], 1), jnp.concatenate([l_high, l_high], 1)], 0
    )
    part_a = jnp.dot(left_a, right_a, preferred_element_type=F32)
    part_b = jnp.dot(left_b, right_b, preferred_element_type=F32)
    total = 6 * chans
    sums = (part_b + part_a[:total]) + part_a[total:]
    cb_real, cb_imag, cp_real, cp_imag, pb_real, pb_imag = [
        sums[i * chans : (i + 1) * chans] for i in range(6)
    ]
    num_real = cp_real * pb_real - cp_imag * pb_imag
    num_imag = cp_real * pb_imag + cp_imag * pb_real
    q_real = cb_real - (num_real * d_real - num_imag * d_imag)
    q_imag = cb_imag - (num_real * d_imag + num_imag * d_real)
    half = group * width
    b_real = (q_real[:, :half] + q_real[:, half:]) * weight
    b_imag = (q_imag[:, :half] - q_imag[:, half:]) * weight
    s_real = b_real * cos_half + b_imag * sin_half
    s_imag = b_imag * cos_half - b_real * sin_half
    for g in range(group):
        cols = slice(g * width, (g + 1) * width)
        out_ref[g, :, :width] = s_real[:, cols]
        out_ref[g, :, width:] = s_imag[:, cols]


def half_spectrum(tables, rates, left, chans, width, group):
    pairs = tables.shape[1]
    steps = pairs // group
    states = rates.shape[0]
    tables = tables.reshape(3, steps, group * width).transpose(1, 0, 2)
    tables = jnp.asarray(tables)
    return pl.pallas_call(
        functools.partial(response_kernel, chans, group, width),
        grid=(steps,),
        in_specs=[
            pl.BlockSpec((1, 3, group * width), lambda i: (i, 0, 0)),
            pl.BlockSpec((states, 3), lambda i: (0, 0)),
            pl.BlockSpec((6 * chans, 2 * states), lambda i: (0, 0)),
        ],
        out_specs=pl.BlockSpec((group, chans, 2 * width), lambda i: (i, 0, 0)),
        out_shape=jax.ShapeDtypeStruct((pairs, chans, 2 * width), F32),
        cost_estimate=pl.CostEstimate(
            flops=pairs * width * chans * states * 48, bytes_accessed=1 << 21, transcendentals=0
        ),
        name="response",
    )(tables, rates, left)


def conv_kernel(
    seq_count, chans, width,
    x_ref, s_ref, t_ref, skip_ref, first_ref, tw_ref, forward_ref, inverse_ref, last_ref,
    out_ref, xf, ar, ai,
):
    pairs = seq_count + 1
    rows = padded(pairs)
    bundle = 4
    for s in range(seq_count):
        xf[s * chans : (s + 1) * chans, :] = x_ref[s].astype(F32)
    tw_cos, tw_sin = tw_ref[0], tw_ref[1]
    for base in range(0, chans, bundle):
        parts = [xf[pl.ds(base + j, seq_count, stride=chans), :] for j in range(bundle)]
        right = jnp.concatenate(parts, 1).astype(BF16)
        right = jnp.concatenate([right, right], 0)
        got = jnp.dot(first_ref[...], right, preferred_element_type=F32)
        for j in range(bundle):
            cols = slice(j * width, (j + 1) * width)
            real, imag = got[:rows, cols], got[rows:, cols]
            ar[pl.ds(base + j, rows, stride=chans), :] = real * tw_cos + imag * tw_sin
            ai[pl.ds(base + j, rows, stride=chans), :] = imag * tw_cos - real * tw_sin

    def filter_rows(source, start, per_loop):
        span = per_loop * chans

        def step(index, carry):
            at = pl.ds(pl.multiple_of(start * chans + index * span, 8), span)
            left = jnp.concatenate([ar[at, :], ai[at, :]], 1).astype(BF16)
            spec = jnp.dot(left, forward_ref[...], preferred_element_type=F32)
            filt = source[pl.ds(index * per_loop, per_loop)].reshape(span, 2 * width)
            x_r, x_i = spec[:, :width], spec[:, width:]
            f_r, f_i = filt[:, :width], filt[:, width:]
            prod = jnp.concatenate([x_r * f_r - x_i * f_i, x_r * f_i + x_i * f_r], 1)
            back = jnp.dot(prod.astype(BF16), inverse_ref[...], preferred_element_type=F32)
            ar[at, :] = back[:, :width]
            ai[at, :] = back[:, width:]
            return carry

        lax.fori_loop(0, source.shape[0] // per_loop, step, 0)

    filter_rows(s_ref, 0, group_of(s_ref.shape[0], 13))
    filter_rows(t_ref, s_ref.shape[0], group_of(t_ref.shape[0], 13))

    for base in range(0, chans, bundle):
        parts = []
        for j in range(bundle):
            real = ar[pl.ds(base + j, rows, stride=chans), :]
            imag = ai[pl.ds(base + j, rows, stride=chans), :]
            parts.append(
                jnp.concatenate(
                    [real * tw_cos - imag * tw_sin, imag * tw_cos + real * tw_sin], 0
                )
            )
        right = jnp.concatenate(parts, 1).astype(BF16)
        got = jnp.dot(last_ref[...], right, preferred_element_type=F32)
        for j in range(bundle):
            at = pl.ds(base + j, seq_count, stride=chans)
            skip = skip_ref[base + j : base + j + 1, :]
            xf[at, :] = got[:, j * width : (j + 1) * width] + skip * xf[at, :]
    for s in range(seq_count):
        pre = xf[s * chans : (s + 1) * chans, :]
        act = 0.5 * pre * (1.0 + lax.erf(pre * math.sqrt(0.5)))
        out_ref[s // 2, :, (s % 2) * width : (s % 2 + 1) * width] = act.astype(BF16)


def filtered(columns, spectrum, skip, seq_count, chans, width):
    pairs = seq_count + 1
    tables = conv_tables(seq_count, width)
    return pl.pallas_call(
        functools.partial(conv_kernel, seq_count, chans, width),
        out_shape=jax.ShapeDtypeStruct((seq_count // 2, chans, 2 * width), BF16),
        scratch_shapes=[
            pltpu.VMEM((seq_count * chans, width), F32),
            pltpu.VMEM((padded(pairs) * chans, width), F32),
            pltpu.VMEM((padded(pairs) * chans, width), F32),
        ],
        cost_estimate=pl.CostEstimate(
            flops=1 << 29, bytes_accessed=1 << 21, transcendentals=1 << 18
        ),
        name="conv",
    )(columns, *spectrum, skip, *tables)


def complex_mul(first, second):
    return (
        first[0] * second[0] - first[1] * second[1],
        first[0] * second[1] + first[1] * second[0],
    )


def left_matrix(coupling, in_own, out_own):
    low = (coupling[0][:, None], coupling[1][:, None])
    low_conj = (low[0], -low[1])
    blocks = []
    for first, second in ((out_own, in_own), (out_own, low), (low_conj, in_own)):
        real, imag = complex_mul(first, second)
        blocks.append(jnp.concatenate([real, -imag], 0).T)
        blocks.append(jnp.concatenate([imag, real], 0).T)
    return jnp.concatenate(blocks, 0)


AXES = ("chip", "core")


def weight_pieces(mix_weight, chip_count):
    chip, core = lax.axis_index("chip"), lax.axis_index("core")
    if chip_count != 16:
        whole = lax.all_gather(mix_weight, "chip", axis=0)
        return [whole], jnp.arange(chip_count, dtype=jnp.int32)
    spots = [(z, y, x, c) for z in range(4) for y in range(2) for x in range(2) for c in range(2)]

    def moved(value, target):
        number = lambda z, y, x, c: ((z * 2 + y) * 2 + x) * 2 + c
        pairs = [(number(*spot), number(*target(*spot))) for spot in spots]
        return lax.ppermute(value, AXES, pairs)

    def near(z, y, x, c):
        return (z, y, 1 - x, c) if c == 0 else (z, 1 - y, x, c)

    def far(z, y, x, c):
        return (z, 1 - y, x, c) if c == 0 else (z, y, 1 - x, c)

    pieces, raised = [], {0: mix_weight}
    for offset, source, lift in ((0, 0, 0), (1, 0, 1), (3, 0, 3), (2, 1, 1)):
        if offset:
            raised[offset] = moved(
                raised[source], lambda z, y, x, c: ((z + lift) % 4, y, x, c)
            )
        block = raised[offset]
        beside = moved(block, near)
        across = moved(block, far)
        corner = moved(beside, far)
        pieces += [value[None] for value in (block, beside, across, corner)]
    slot = jnp.arange(16, dtype=jnp.int32)
    kind = slot % 4
    twist = jnp.where(core == 0, kind, jnp.where((kind == 1) | (kind == 2), 3 - kind, kind))
    offset = jnp.where(slot < 8, slot // 4, 5 - slot // 4)
    order = ((chip // 4 + 4 - offset) % 4) * 4 + jnp.bitwise_xor(chip % 4, twist)
    return pieces, order.astype(jnp.int32)


def mix_kernel(width, order_ref, act_ref, *refs):
    *piece_refs, theirs_ref, ours_ref, left = refs
    chips, chans, _ = act_ref.shape
    core = order_ref[chips]
    theirs = pl.multiple_of((1 - core) * width, width)
    ours = pl.multiple_of(core * width, width)
    for j in range(chips):
        rows = slice(j * chans, (j + 1) * chans)
        left[rows, :width] = act_ref[order_ref[j], :, pl.ds(theirs, width)]
        left[rows, width:] = act_ref[order_ref[j], :, pl.ds(ours, width)]
    tokens = left[...].T
    tile = 512
    for col in range(0, theirs_ref.shape[1], tile):
        parts = []
        for piece in piece_refs:
            rows = piece.shape[0] * piece.shape[1]
            parts.append(piece[:, :, col : col + tile].reshape(rows, tile))
        block = jnp.concatenate(parts, 0)
        total = jnp.dot(tokens, block, preferred_element_type=F32)
        theirs_ref[:, col : col + tile] = total[:width].astype(BF16)
        ours_ref[:, col : col + tile] = total[width:]


def mixed(act, pieces, order, core, width):
    chips, chans, both = act.shape
    cols = pieces[0].shape[-1]
    table = jnp.where(jnp.arange(chips + 1) < chips, jnp.pad(order, (0, 1)), core)
    return pl.pallas_call(
        functools.partial(mix_kernel, width),
        in_specs=[pl.BlockSpec(memory_space=pltpu.SMEM)]
        + [pl.BlockSpec(memory_space=pltpu.VMEM)] * (1 + len(pieces)),
        out_specs=[pl.BlockSpec(memory_space=pltpu.VMEM)] * 2,
        out_shape=[
            jax.ShapeDtypeStruct((width, cols), BF16),
            jax.ShapeDtypeStruct((width, cols), F32),
        ],
        scratch_shapes=[pltpu.VMEM((chips * chans, both), BF16)],
        cost_estimate=pl.CostEstimate(
            flops=2 * both * chips * chans * cols,
            bytes_accessed=chips * chans * cols * 2,
            transcendentals=0,
        ),
        name="mix",
    )(table.astype(jnp.int32), act, *pieces)


def finish_kernel(ours_ref, arrived_ref, out_ref):
    cols = out_ref.shape[1]
    for col in range(0, cols, 256):
        at, gate_at = slice(col, col + 256), slice(cols + col, cols + col + 256)
        value = ours_ref[:, at] + arrived_ref[:, at].astype(F32)
        gate = ours_ref[:, gate_at] + arrived_ref[:, gate_at].astype(F32)
        out_ref[:, at] = (value * jax.nn.sigmoid(gate)).astype(BF16)


def finished(ours, arrived):
    rows, cols = ours.shape
    return pl.pallas_call(
        finish_kernel,
        in_specs=[pl.BlockSpec(memory_space=pltpu.VMEM)] * 2,
        out_specs=pl.BlockSpec(memory_space=pltpu.VMEM),
        out_shape=jax.ShapeDtypeStruct((rows, cols // 2), BF16),
        cost_estimate=pl.CostEstimate(
            flops=rows * cols * 4, bytes_accessed=rows * cols * 7, transcendentals=rows * cols
        ),
        name="finish",
    )(ours, arrived)


def shards(tokens, state_rates, coupling, in_proj, out_proj, skip_gain, mix_weight):
    chip_count = lax.axis_size("chip")
    seq_count = chip_count * lax.axis_size("core")
    core = lax.axis_index("core")
    place = lax.axis_index(AXES)
    width, channels = tokens.shape
    chans = channels // seq_count
    columns = tokens.T.reshape(seq_count, chans, width)
    columns = lax.all_to_all(columns, AXES, 0, 0)
    pieces, order = weight_pieces(mix_weight, chip_count)
    skip = lax.dynamic_slice_in_dim(skip_gain, place * chans, chans, 0)[:, None]
    in_own = lax.dynamic_slice_in_dim(in_proj, place * chans, chans, 2)
    out_own = lax.dynamic_slice_in_dim(out_proj, place * chans, chans, 2)
    left = left_matrix(coupling, in_own, out_own)
    power = coupling[0] * coupling[0] + coupling[1] * coupling[1]
    rates = jnp.stack([state_rates[0], state_rates[1], power], 1)
    tables = half_angles(seq_count, width)
    pairs = tables.shape[1]
    group = group_of(pairs, 6)
    cut = -(-pairs // group // 2) * group
    spectrum = []
    for part in (tables[:, :cut], tables[:, cut:]):
        spectrum.append(half_spectrum(part, rates, left, chans, width, group))
    activation = filtered(columns, spectrum, skip, seq_count, chans, width)
    act = lax.all_to_all(activation, "chip", 0, 0)
    theirs, ours = mixed(act, pieces, order, core, width)
    arrived = lax.ppermute(theirs, "core", [(0, 1), (1, 0)])
    return finished(ours, arrived)


def solution(mesh):
    groups, seq = mesh.shape["groups"], mesh.shape["seq"]
    chips = Mesh(mesh.devices.reshape(groups, seq // 2, 2), ("groups", *AXES))
    rows = ("groups", *AXES)

    placed = (P(rows, None), P(), P(), P(), P(), P(), P(AXES, None))
    return jax.shard_map(
        shards, mesh=chips, in_specs=placed, out_specs=P(rows, None), check_vma=False
    )
```

```python
import functools
import math

import jax
import jax.numpy as jnp
import numpy as np
from jax import lax
from jax.experimental import pallas as pl
from jax.experimental.pallas import tpu as pltpu
from jax.sharding import Mesh, PartitionSpec as P


F32 = jnp.float32
BF16 = jnp.bfloat16


def padded(count):
    return -(-count // 8) * 8


def group_of(count, most):
    return max(g for g in range(1, most + 1) if count % g == 0)


def half_angles(seq_count, tok_rows):
    full_len = 2 * seq_count * tok_rows
    freq = np.arange(seq_count + 1)[:, None] + 2 * seq_count * np.arange(tok_rows)[None, :]
    wrapped = np.where(freq > full_len // 2, freq - full_len, freq).astype(np.float32)
    half = wrapped * np.float32(-2.0 * math.pi / full_len) * np.float32(0.5)
    half = half.astype(np.float64)
    weight = np.full((seq_count + 1, 1), 2.0)
    weight[0] = weight[-1] = 1.0
    weight = np.broadcast_to(weight / (2.0 * full_len), half.shape)
    return np.stack([np.cos(half), np.sin(half), weight]).astype(np.float32)


def split_table(table):
    high = table.astype(jnp.bfloat16).astype(np.float64)
    return high.astype(np.float32), (table - high).astype(np.float32)


def conv_tables(seq_count, tok_rows):
    pairs = seq_count + 1
    rows = padded(pairs)
    full_len = 2 * seq_count * tok_rows
    outer = 2.0 * np.pi * np.outer(np.arange(pairs), np.arange(seq_count)) / (2 * seq_count)
    first = np.zeros((2 * rows, seq_count))
    first[:pairs] = np.cos(outer)
    first[rows : rows + pairs] = -np.sin(outer)
    first = np.concatenate(split_table(first), 1)
    last = np.zeros((seq_count, 2 * rows))
    last[:, :pairs] = np.cos(outer).T
    last[:, rows : rows + pairs] = -np.sin(outer).T
    turn = 2.0 * np.pi * np.outer(np.arange(pairs), np.arange(tok_rows)) / full_len
    twiddle = np.zeros((2, rows, tok_rows))
    twiddle[0, :pairs] = np.cos(turn)
    twiddle[1, :pairs] = np.sin(turn)
    inner = 2.0 * np.pi * np.outer(np.arange(tok_rows), np.arange(tok_rows)) / tok_rows
    cosine, sine = np.cos(inner), np.sin(inner)
    forward = np.block([[cosine, -sine], [sine, cosine]])
    inverse = np.block([[cosine, sine], [-sine, cosine]])
    turns = np.concatenate(split_table(twiddle.reshape(2 * rows, tok_rows)), 1)
    parts, places, at = [], [], 0
    for table in (first, turns, last, forward, inverse):
        height = -(-table.shape[0] // 16) * 16
        filled = np.zeros((height, 2 * tok_rows))
        filled[: table.shape[0], : table.shape[1]] = table
        parts.append(filled)
        places.append((at, *table.shape))
        at += height
    return jnp.asarray(np.concatenate(parts, 0), BF16), tuple(places)


def complex_mul(first, second):
    return (
        first[0] * second[0] - first[1] * second[1],
        first[0] * second[1] + first[1] * second[0],
    )


def thirds(value):
    high = value.astype(BF16)
    rest = value - high.astype(F32)
    middle = rest.astype(BF16)
    low = (rest - middle.astype(F32)).astype(BF16)
    return high, middle, low


def column_of(row):
    size = row.shape[1]
    if size < 128:
        row = jnp.concatenate([row, jnp.zeros((1, 128 - size), row.dtype)], 1)
    return jnp.broadcast_to(row, (8, 128)).T[:size, 0:1]


def response_kernel(
    group, width, tab_ref, rates_ref, low_ref, in_ref, out_proj_ref, out_ref, left_a, left_b, side
):
    _, chans = in_ref.shape[1:]
    total = 6 * chans

    @pl.when(pl.program_id(0) == 0)
    def _():
        low = (low_ref[0:1, :], low_ref[1:2, :])
        low_conj = (low[0], -low[1])
        side[:, 0:1] = column_of(-rates_ref[0:1, :])
        side[:, 1:2] = column_of(rates_ref[1:2, :])
        side[:, 2:3] = column_of(low[0] * low[0] + low[1] * low[1])
        in_pair = (in_ref[0].T, in_ref[1].T)
        out_pair = (out_proj_ref[0].T, out_proj_ref[1].T)
        blocks = []
        for first, second in ((out_pair, in_pair), (out_pair, low), (low_conj, in_pair)):
            real, imag = complex_mul(first, second)
            blocks.append(jnp.concatenate([real, -imag], 1))
            blocks.append(jnp.concatenate([imag, real], 1))
        high, middle, low_part = thirds(jnp.concatenate(blocks, 0))
        left_a[:total, :] = jnp.concatenate([middle, middle], 1)
        left_a[total:, :] = jnp.concatenate([high, high], 1)
        left_b[...] = jnp.concatenate([high, low_part], 1)

    cos_half = tab_ref[0, 0:1, :]
    sin_half = tab_ref[0, 1:2, :]
    weight = tab_ref[0, 2:3, :]
    cos_two = jnp.concatenate([cos_half, cos_half], 1)
    sin_two = jnp.concatenate([sin_half, -sin_half], 1)
    decay = side[:, 0:1]
    spin = side[:, 1:2]
    power = side[:, 2:3]
    real_part = cos_two * decay
    imag_part = -(2.0 * sin_two + cos_two * spin)
    inv_norm = 1.0 / (real_part * real_part + imag_part * imag_part)
    v_real = real_part * inv_norm
    v_imag = -imag_part * inv_norm
    pp_real = jnp.sum(v_real * power, axis=0, keepdims=True)
    pp_imag = jnp.sum(v_imag * power, axis=0, keepdims=True)
    den_real = 1.0 + cos_two * pp_real
    den_imag = cos_two * pp_imag
    den_inv = cos_two / (den_real * den_real + den_imag * den_imag)
    d_real = den_real * den_inv
    d_imag = -den_imag * den_inv
    v_high, v_mid, v_low = thirds(jnp.concatenate([v_real, v_imag], 0))
    right_a = jnp.concatenate([v_high, v_mid], 0)
    right_b = jnp.concatenate([v_low, v_high], 0)
    part_a = jnp.dot(left_a[...], right_a, preferred_element_type=F32)
    part_b = jnp.dot(left_b[...], right_b, preferred_element_type=F32)
    sums = (part_b + part_a[:total]) + part_a[total:]
    cb_real, cb_imag, cp_real, cp_imag, pb_real, pb_imag = [
        sums[i * chans : (i + 1) * chans] for i in range(6)
    ]
    num_real = cp_real * pb_real - cp_imag * pb_imag
    num_imag = cp_real * pb_imag + cp_imag * pb_real
    q_real = cb_real - (num_real * d_real - num_imag * d_imag)
    q_imag = cb_imag - (num_real * d_imag + num_imag * d_real)
    half = group * width
    b_real = (q_real[:, :half] + q_real[:, half:]) * weight
    b_imag = (q_imag[:, :half] - q_imag[:, half:]) * weight
    s_real = b_real * cos_half + b_imag * sin_half
    s_imag = b_imag * cos_half - b_real * sin_half
    for g in range(group):
        cols = slice(g * width, (g + 1) * width)
        out_ref[g, :, :width] = s_real[:, cols]
        out_ref[g, :, width:] = s_imag[:, cols]


def half_spectrum(tables, start, steps, rates, low, in_own, out_own, width, group):
    pairs = steps * group
    states, chans = in_own.shape[1:]
    whole = lambda value: pl.BlockSpec(value.shape, lambda i: (0,) * value.ndim)
    return pl.pallas_call(
        functools.partial(response_kernel, group, width),
        grid=(steps,),
        in_specs=[
            pl.BlockSpec((1, 3, group * width), lambda i: (i + start, 0, 0)),
            whole(rates),
            whole(low),
            whole(in_own),
            whole(out_own),
        ],
        out_specs=pl.BlockSpec((group, chans, 2 * width), lambda i: (i, 0, 0)),
        out_shape=jax.ShapeDtypeStruct((pairs, chans, 2 * width), F32),
        scratch_shapes=[
            pltpu.VMEM((12 * chans, 4 * states), BF16),
            pltpu.VMEM((6 * chans, 4 * states), BF16),
            pltpu.VMEM((states, 128), F32),
        ],
        cost_estimate=pl.CostEstimate(
            flops=pairs * width * chans * states * 48, bytes_accessed=1 << 21, transcendentals=0
        ),
        compiler_params=pltpu.CompilerParams(vmem_limit_bytes=12 << 20),
        name="response",
    )(tables, rates, low, in_own, out_own)


def conv_kernel(seq_count, chans, width, places, x_ref, *refs):
    s_refs, (skip_ref, tab_ref, out_ref, xf, ar, ai) = refs[:PARTS], refs[PARTS:]
    pairs = seq_count + 1
    rows = padded(pairs)
    bundle = 4
    for s in range(seq_count):
        xf[s * chans : (s + 1) * chans, :] = x_ref[s].astype(F32)
    first, turns, last, forward, inverse = [
        (lambda at=at, height=height, wide=wide: tab_ref[at : at + height, :wide])
        for at, height, wide in places
    ]
    turn = turns().astype(F32)
    turn = turn[:, :width] + turn[:, width:]
    tw_cos, tw_sin = turn[:rows], turn[rows:]
    skip_col = column_of(skip_ref[...])
    for base in range(0, chans, bundle):
        parts = [xf[pl.ds(base + j, seq_count, stride=chans), :] for j in range(bundle)]
        right = jnp.concatenate(parts, 1).astype(BF16)
        right = jnp.concatenate([right, right], 0)
        got = jnp.dot(first(), right, preferred_element_type=F32)
        for j in range(bundle):
            cols = slice(j * width, (j + 1) * width)
            real, imag = got[:rows, cols], got[rows:, cols]
            ar[pl.ds(base + j, rows, stride=chans), :] = real * tw_cos + imag * tw_sin
            ai[pl.ds(base + j, rows, stride=chans), :] = imag * tw_cos - real * tw_sin

    def filter_rows(source, start, per_loop):
        span = per_loop * chans

        def step(index, carry):
            at = pl.ds(pl.multiple_of(start * chans + index * span, 8), span)
            left = jnp.concatenate([ar[at, :], ai[at, :]], 1).astype(BF16)
            spec = jnp.dot(left, forward(), preferred_element_type=F32)
            filt = source[pl.ds(index * per_loop, per_loop)].reshape(span, 2 * width)
            x_r, x_i = spec[:, :width], spec[:, width:]
            f_r, f_i = filt[:, :width], filt[:, width:]
            prod = jnp.concatenate([x_r * f_r - x_i * f_i, x_r * f_i + x_i * f_r], 1)
            back = jnp.dot(prod.astype(BF16), inverse(), preferred_element_type=F32)
            ar[at, :] = back[:, :width]
            ai[at, :] = back[:, width:]
            return carry

        lax.fori_loop(0, source.shape[0] // per_loop, step, 0)

    start = 0
    for source in s_refs:
        filter_rows(source, start, group_of(source.shape[0], 13))
        start += source.shape[0]

    for base in range(0, chans, bundle):
        parts = []
        for j in range(bundle):
            real = ar[pl.ds(base + j, rows, stride=chans), :]
            imag = ai[pl.ds(base + j, rows, stride=chans), :]
            parts.append(
                jnp.concatenate(
                    [real * tw_cos - imag * tw_sin, imag * tw_cos + real * tw_sin], 0
                )
            )
        right = jnp.concatenate(parts, 1).astype(BF16)
        got = jnp.dot(last(), right, preferred_element_type=F32)
        for j in range(bundle):
            at = pl.ds(base + j, seq_count, stride=chans)
            skip = skip_col[base + j : base + j + 1, :]
            xf[at, :] = got[:, j * width : (j + 1) * width] + skip * xf[at, :]
    for s in range(seq_count):
        pre = xf[s * chans : (s + 1) * chans, :]
        act = 0.5 * pre * (1.0 + lax.erf(pre * math.sqrt(0.5)))
        out_ref[s // 2, :, (s % 2) * width : (s % 2 + 1) * width] = act.astype(BF16)


def filtered(columns, spectrum, skip, seq_count, chans, width):
    pairs = seq_count + 1
    tables, places = conv_tables(seq_count, width)
    return pl.pallas_call(
        functools.partial(conv_kernel, seq_count, chans, width, places),
        in_specs=[pl.BlockSpec(memory_space=pltpu.VMEM)] * (3 + PARTS),
        out_specs=pl.BlockSpec(memory_space=pltpu.VMEM),
        out_shape=jax.ShapeDtypeStruct((seq_count // 2, chans, 2 * width), BF16),
        scratch_shapes=[
            pltpu.VMEM((seq_count * chans, width), F32),
            pltpu.VMEM((padded(pairs) * chans, width), F32),
            pltpu.VMEM((padded(pairs) * chans, width), F32),
        ],
        cost_estimate=pl.CostEstimate(
            flops=1 << 29, bytes_accessed=1 << 21, transcendentals=1 << 18
        ),
        compiler_params=pltpu.CompilerParams(vmem_limit_bytes=14 << 20),
        name="conv",
    )(columns, *spectrum, skip, tables)


AXES = ("chip", "core")
PARTS = 1


def weight_pieces(mix_weight, chip_count):
    chip, core = lax.axis_index("chip"), lax.axis_index("core")
    if chip_count != 16:
        whole = lax.all_gather(mix_weight, "chip", axis=0)
        return [whole], jnp.arange(chip_count, dtype=jnp.int32)
    spots = [(z, y, x, c) for z in range(4) for y in range(2) for x in range(2) for c in range(2)]

    def moved(value, target):
        number = lambda z, y, x, c: ((z * 2 + y) * 2 + x) * 2 + c
        pairs = [(number(*spot), number(*target(*spot))) for spot in spots]
        return lax.ppermute(value, AXES, pairs)

    def near(z, y, x, c):
        return (z, y, 1 - x, c) if c == 0 else (z, 1 - y, x, c)

    def far(z, y, x, c):
        return (z, 1 - y, x, c) if c == 0 else (z, y, 1 - x, c)

    pieces, raised = [], {0: mix_weight}
    for offset, source, lift in ((0, 0, 0), (1, 0, 1), (3, 0, 3), (2, 1, 1)):
        if offset:
            raised[offset] = moved(
                raised[source], lambda z, y, x, c: ((z + lift) % 4, y, x, c)
            )
        block = raised[offset]
        beside = moved(block, near)
        across = moved(block, far)
        corner = moved(beside, far)
        pieces += [value[None] for value in (block, beside, across, corner)]
    slot = jnp.arange(16, dtype=jnp.int32)
    kind = slot % 4
    twist = jnp.where(core == 0, kind, jnp.where((kind == 1) | (kind == 2), 3 - kind, kind))
    offset = jnp.where(slot < 8, slot // 4, 5 - slot // 4)
    order = ((chip // 4 + 4 - offset) % 4) * 4 + jnp.bitwise_xor(chip % 4, twist)
    return pieces, order.astype(jnp.int32)


def mix_kernel(width, order_ref, act_ref, *refs):
    *piece_refs, theirs_ref, ours_ref, left = refs
    chips, chans, _ = act_ref.shape
    core = order_ref[chips]
    theirs = pl.multiple_of((1 - core) * width, width)
    ours = pl.multiple_of(core * width, width)
    for j in range(chips):
        rows = slice(j * chans, (j + 1) * chans)
        left[rows, :width] = act_ref[order_ref[j], :, pl.ds(theirs, width)]
        left[rows, width:] = act_ref[order_ref[j], :, pl.ds(ours, width)]
    tokens = left[...].T
    tile = 512
    for col in range(0, theirs_ref.shape[1], tile):
        parts = []
        for piece in piece_refs:
            rows = piece.shape[0] * piece.shape[1]
            parts.append(piece[:, :, col : col + tile].reshape(rows, tile))
        block = jnp.concatenate(parts, 0)
        total = jnp.dot(tokens, block, preferred_element_type=F32)
        theirs_ref[:, col : col + tile] = total[:width].astype(BF16)
        ours_ref[:, col : col + tile] = total[width:]


def mixed(act, pieces, order, core, width):
    chips, chans, both = act.shape
    cols = pieces[0].shape[-1]
    table = jnp.where(jnp.arange(chips + 1) < chips, jnp.pad(order, (0, 1)), core)
    return pl.pallas_call(
        functools.partial(mix_kernel, width),
        in_specs=[pl.BlockSpec(memory_space=pltpu.SMEM)]
        + [pl.BlockSpec(memory_space=pltpu.VMEM)] * (1 + len(pieces)),
        out_specs=[pl.BlockSpec(memory_space=pltpu.VMEM)] * 2,
        out_shape=[
            jax.ShapeDtypeStruct((width, cols), BF16),
            jax.ShapeDtypeStruct((width, cols), F32),
        ],
        scratch_shapes=[pltpu.VMEM((chips * chans, both), BF16)],
        cost_estimate=pl.CostEstimate(
            flops=2 * both * chips * chans * cols,
            bytes_accessed=chips * chans * cols * 2,
            transcendentals=0,
        ),
        compiler_params=pltpu.CompilerParams(vmem_limit_bytes=24 << 20),
        name="mix",
    )(table.astype(jnp.int32), act, *pieces)


def finish_kernel(ours_ref, arrived_ref, out_ref):
    cols = out_ref.shape[1]
    for col in range(0, cols, 256):
        at, gate_at = slice(col, col + 256), slice(cols + col, cols + col + 256)
        value = ours_ref[:, at] + arrived_ref[:, at].astype(F32)
        gate = ours_ref[:, gate_at] + arrived_ref[:, gate_at].astype(F32)
        out_ref[:, at] = (value * (0.5 + 0.5 * jnp.tanh(0.5 * gate))).astype(BF16)


def finished(ours, arrived):
    rows, cols = ours.shape
    return pl.pallas_call(
        finish_kernel,
        in_specs=[pl.BlockSpec(memory_space=pltpu.VMEM)] * 2,
        out_specs=pl.BlockSpec(memory_space=pltpu.VMEM),
        out_shape=jax.ShapeDtypeStruct((rows, cols // 2), BF16),
        cost_estimate=pl.CostEstimate(
            flops=rows * cols * 4, bytes_accessed=rows * cols * 7, transcendentals=rows * cols
        ),
        compiler_params=pltpu.CompilerParams(vmem_limit_bytes=8 << 20),
        name="finish",
    )(ours, arrived)


def shards(tokens, state_rates, coupling, in_proj, out_proj, skip_gain, mix_weight):
    chip_count = lax.axis_size("chip")
    seq_count = chip_count * lax.axis_size("core")
    core = lax.axis_index("core")
    place = lax.axis_index(AXES)
    width, channels = tokens.shape
    chans = channels // seq_count
    columns = tokens.T.reshape(seq_count, chans, width)
    columns = lax.all_to_all(columns, AXES, 0, 0)
    pieces, order = weight_pieces(mix_weight, chip_count)
    skip = lax.dynamic_slice_in_dim(skip_gain, place * chans, chans, 0)[None]
    in_own = lax.dynamic_slice_in_dim(in_proj, place * chans, chans, 2)
    out_own = lax.dynamic_slice_in_dim(out_proj, place * chans, chans, 2)
    in_own, out_own, skip = lax.optimization_barrier((in_own, out_own, skip))
    tables = half_angles(seq_count, width)
    group = group_of(tables.shape[1], 6)
    steps = tables.shape[1] // group
    tables = tables.reshape(3, steps, group * width).transpose(1, 0, 2)
    tables = jnp.asarray(tables)
    cut = -(-steps // PARTS)
    spectrum = []
    for index in range(PARTS):
        start = index * cut
        count = min(cut, steps - start)
        spectrum.append(
            half_spectrum(
                tables, start, count, state_rates, coupling, in_own, out_own, width, group
            )
        )
    activation = filtered(columns, spectrum, skip, seq_count, chans, width)
    act = lax.all_to_all(activation, "chip", 0, 0)
    theirs, ours = mixed(act, pieces, order, core, width)
    arrived = lax.ppermute(theirs, "core", [(0, 1), (1, 0)])
    return finished(ours, arrived)


def solution(mesh):
    groups, seq = mesh.shape["groups"], mesh.shape["seq"]
    chips = Mesh(mesh.devices.reshape(groups, seq // 2, 2), ("groups", *AXES))
    rows = ("groups", *AXES)

    placed = (P(rows, None), P(), P(), P(), P(), P(), P(AXES, None))
    return jax.shard_map(
        shards, mesh=chips, in_specs=placed, out_specs=P(rows, None), check_vma=False
    )
```
